512 devices in a mesh: rep: 16 (over z_hi, x), shard: 32 (over z_lo, y, core).
Axes of the slice: x: 4, y: 4, z: 16 (z_hi: 4, z_lo: 4; z = z_hi * 4 + z_lo), core: 2. Of those that a mesh axis runs over, the one named last changes fastest.
Arguments:
- slow_weights: float32 [16, 256, 8192], P('rep', 'shard'), may hold values from -0.12 to 0.12
- outer_momentum: float32 [16, 256, 8192], P('rep', 'shard'), may hold values from -0.018 to 0.018
- adam_first: float32 [16, 256, 8192], P('rep', 'shard'), may hold values from -1 to 1
- adam_second: float32 [16, 256, 8192], P('rep', 'shard'), may hold values from 0 to 1, as said below
- gradients: bfloat16 [4, 4, 16, 256, 8192], P(None, None, 'rep', 'shard'), may hold values from -1000 to 1000, as said below
- pair_mask: int32 [4], replicated, may hold values from 1 to 8, as said below
Outputs:
- new_slow: float32 [16, 256, 8192], P('rep', 'shard')
- new_momentum: float32 [16, 256, 8192], P('rep', 'shard')
- new_first: float32 [16, 256, 8192], P('rep', 'shard')
- new_second: float32 [16, 256, 8192], P('rep', 'shard')
The draws below stay inside these ranges and needn't reach their ends.
Inputs may be any that keep to these rules, and one draw needn't show every extreme that they name: In outer step t replica r is matched with replica r XOR pair_mask[t] (bitwise exclusive or); 16 is a power of two, and every pair_mask[t] is a single power of two. Every bit of 15 occurs in some outer step; in which order is drawn anew. `gradients`: gradients of all inner updates. `adam_second`: second moments, positive.
All inputs are finite; a program needn't handle non-finite values.
Results may differ from the reference program's by a relative error of at most 0.0018.
Values may be sent and summed in bfloat16 or wider, within the bound.
No kernel may reach another device: no remote copies, remote signals or barrier semaphores. Data moves between devices by JAX's collectives and lax.ppermute only.
A program may use at most 64 MiB of HBM per device.

```python
import math
import jax
import jax.numpy as jnp
from jax import lax

D = 8192
OUTER = 4
INNER = 4
ROWS = 256
REPLICAS = 16


def draw_gradients(key, part):
    keys = jax.random.split(jax.random.fold_in(key, 11), 5)
    shape = (OUTER, INNER, REPLICAS, ROWS, D)
    rising = jnp.exp(math.log(3.0) * jnp.arange(ROWS, dtype=jnp.float32) / ROWS)
    step_scale = jnp.exp(jax.random.uniform(keys[0], (OUTER, INNER, REPLICAS, 1, 1), jnp.float32, math.log(0.3), math.log(3.0)))
    row_scale = jnp.exp(jax.random.uniform(keys[1], (OUTER, INNER, REPLICAS, ROWS, 1), jnp.float32, 0.0, math.log(10.0)))
    values = jnp.clip(jax.random.normal(keys[4], shape, jnp.float32), -4.0, 4.0)
    scaled = jnp.clip(values * step_scale * row_scale * rising[:, None], -1000.0, 1000.0)
    return scaled.astype(jnp.bfloat16)


def draw_adam_first(key, part):
    shape = (REPLICAS, ROWS, D)
    level = 0.3 / math.sqrt(ROWS * D)
    values = jnp.clip(jax.random.normal(jax.random.fold_in(key, 22), shape, jnp.float32), -4.0, 4.0)
    return (values * level).astype(jnp.float32)


def draw_adam_second(key, part):
    shape = (REPLICAS, ROWS, D)
    level = 1.0 / (ROWS * D)
    logs = jax.random.uniform(jax.random.fold_in(key, 32), shape, jnp.float32, math.log(0.1), math.log(10.0))
    return (jnp.exp(logs) * level).astype(jnp.float32)


def draw_pair_mask(key, part):
    bit_count = REPLICAS.bit_length() - 1
    order = jax.random.permutation(jax.random.fold_in(key, 41), bit_count).astype(jnp.int32)
    picks = order[jnp.arange(OUTER, dtype=jnp.int32) % bit_count]
    return jnp.left_shift(jnp.ones((OUTER,), jnp.int32), picks).astype(jnp.int32)


def level_of(key, shape, cuts, smallest, high):
    loudness = 1.0
    for axis_at, parts in cuts:
        draws = jax.random.uniform(jax.random.fold_in(jax.random.fold_in(key, 6), axis_at), (parts,), jnp.float32, smallest / len(cuts), high / len(cuts))
        loudness = loudness * jnp.repeat(jnp.exp(draws), shape[axis_at] // parts).reshape((-1,) + (1,) * (len(shape) - 1 - axis_at))
    return loudness


def normal_values(key, shape, spread, bound, pieces=(), held_as=jnp.bfloat16):
    level = level_of(key, shape, pieces, -0.22, 0.18) if pieces else 1.0
    values = jax.random.normal(key, shape, jnp.float32) * spread * level
    return jnp.minimum(jnp.maximum(values, -bound), bound).astype(held_as)


def setup_inputs(seed: int = 0) -> dict:
    key_of = jax.random.split(jax.random.key(seed), 7)
    return {
        "slow_weights": normal_values(key_of[0], (REPLICAS, ROWS, D), 0.02, 0.12, ((0, 16), (1, 32)), jnp.float32),
        "outer_momentum": normal_values(key_of[1], (REPLICAS, ROWS, D), 0.003, 0.018, ((0, 16), (1, 32)), jnp.float32),
        "adam_first": draw_adam_first(jax.random.fold_in(key_of[6], 71), 0),
        "adam_second": draw_adam_second(jax.random.fold_in(key_of[6], 71), 0),
        "gradients": draw_gradients(jax.random.fold_in(key_of[6], 71), 0),
        "pair_mask": draw_pair_mask(jax.random.fold_in(key_of[6], 71), 0),
    }


clip_limit = 1.0
beta_one = 0.9
beta_two = 0.95
adam_eps = 1e-08
inner_rate = 0.001
decay_rate = 0.1
outer_rate = 0.7
momentum_rate = 0.9
mix_rate = 0.25

def reference(slow_weights, outer_momentum, adam_first, adam_second, gradients, pair_mask):
    slow_now = slow_weights
    momentum = outer_momentum
    moment_one = adam_first
    moment_two = adam_second
    replicas = jnp.arange(REPLICAS, dtype=jnp.int32)
    for outer_step in range(OUTER):
        fast_weights = slow_now
        for inner_step in range(INNER):
            gradient = gradients[outer_step, inner_step].astype(jnp.float32)
            square_sum = lax.optimization_barrier(jnp.sum(gradient * gradient, axis=(1, 2), keepdims=True))
            factor = clip_limit / jnp.maximum(jnp.sqrt(square_sum), clip_limit)
            clipped = factor * gradient
            moment_one = beta_one * moment_one + (1.0 - beta_one) * clipped
            moment_two = beta_two * moment_two + (1.0 - beta_two) * clipped * clipped
            fast_weights = fast_weights - inner_rate * (moment_one / (jnp.sqrt(moment_two) + adam_eps) + decay_rate * fast_weights)
        pseudo_grad = lax.optimization_barrier((slow_now - fast_weights).astype(jnp.bfloat16))
        sent_slow = slow_now.astype(jnp.bfloat16)
        partner = jnp.bitwise_xor(replicas, pair_mask[outer_step]).astype(jnp.int32)
        other_pseudo = jnp.take(pseudo_grad, partner, axis=0).astype(jnp.float32)
        other_slow = jnp.take(sent_slow, partner, axis=0).astype(jnp.float32)
        average = 0.5 * (pseudo_grad.astype(jnp.float32) + other_pseudo)
        momentum = momentum_rate * momentum + average
        slow_now = slow_now + mix_rate * (other_slow - slow_now) - outer_rate * (average + momentum_rate * momentum)
    return (slow_now, momentum, moment_one, moment_two)
```

```python
from functools import partial
from itertools import permutations

import jax
import jax.numpy as jnp
from jax import lax
from jax.experimental import pallas as pl
from jax.experimental.pallas import tpu as pltpu
from jax.sharding import Mesh
from jax.sharding import PartitionSpec as P

SHARD = ("shard_0", "shard_1", "shard_2")
LANES = 128

clip_limit = 1.0
beta_one = 0.9
beta_two = 0.95
adam_eps = 1e-08
inner_rate = 0.001
decay_rate = 0.1
outer_rate = 0.7
momentum_rate = 0.9
mix_rate = 0.25
kept = 1.0 - inner_rate * decay_rate
tiny = 1.2e-38
VMEM = pl.BlockSpec(memory_space=pltpu.VMEM)
SMEM = pl.BlockSpec(memory_space=pltpu.SMEM)
PARAMS = pltpu.CompilerParams(vmem_limit_bytes=8 * 1024 * 1024)


def chunked(columns, width, body):
    @pl.loop(0, columns // width)
    def _(at):
        body(pl.ds(pl.multiple_of(at * width, width), width))


def squares_kernel(mask_ref, gradient_ref, slow_ref, branch_ref, sums_ref, sent_ref, total_ref):
    steps, rows, columns = gradient_ref.shape
    bits = [(mask_ref[t] >> 1) - (mask_ref[t] >> 3) for t in range(4)]
    branch_ref[0] = bits[0]
    branch_ref[1] = (
        bits[0] * 6
        + (bits[1] - (bits[1] > bits[0]).astype(jnp.int32)) * 2
        + (bits[2] > bits[3]).astype(jnp.int32)
    )
    total_ref[...] = jnp.zeros_like(total_ref)

    def body(where):
        sent_ref[:, where] = slow_ref[:, where].astype(jnp.bfloat16)
        for step in range(steps):
            value = gradient_ref[step, :, where].astype(jnp.float32)
            square = value * value
            total_ref[step] += sum(
                square[:, i * LANES : (i + 1) * LANES] for i in range(square.shape[1] // LANES)
            )

    chunked(columns, 1024, body)
    lane = lax.broadcasted_iota(jnp.int32, (1, LANES), 1)
    line = jnp.zeros((1, LANES), jnp.float32)
    for step in range(steps):
        line = jnp.where(lane == step, jnp.sum(total_ref[step]), line)
    for copy in range(sums_ref.shape[0]):
        sums_ref[copy] = line


def squares(pair_mask, gradients, slow, copies):
    steps = gradients.shape[0]
    return pl.pallas_call(
        squares_kernel,
        out_shape=(
            jax.ShapeDtypeStruct((2,), jnp.int32),
            jax.ShapeDtypeStruct((copies, 1, LANES), jnp.float32),
            jax.ShapeDtypeStruct(slow.shape, jnp.bfloat16),
        ),
        in_specs=[SMEM, VMEM, VMEM],
        out_specs=(SMEM, VMEM, VMEM),
        scratch_shapes=[pltpu.VMEM((steps, 8, LANES), jnp.float32)],
        compiler_params=PARAMS,
        name="squares",
    )(pair_mask, gradients, slow)


def adam_kernel(sums_ref, gradient_ref, one_ref, two_ref, *outs):
    moved_refs, (one_out, two_out) = outs[:4], outs[4:]
    steps, rows, columns = gradient_ref.shape
    square_sum = jnp.sum(sums_ref[...], axis=0)
    factor = clip_limit / jnp.maximum(jnp.sqrt(square_sum), clip_limit)
    lane = lax.broadcasted_iota(jnp.int32, (1, LANES), 1)
    factors = [jnp.sum(jnp.where(lane == step, factor, 0.0)) for step in range(steps)]
    inner = steps // len(moved_refs)

    def body(where):
        one, two = one_ref[:, where], two_ref[:, where]
        for outer, moved_ref in enumerate(moved_refs):
            moved = None
            for step in range(outer * inner, outer * inner + inner):
                value = gradient_ref[step, :, where].astype(jnp.float32)
                scale = factors[step]
                one = beta_one * one + ((1.0 - beta_one) * scale) * value
                two = beta_two * two + ((1.0 - beta_two) * scale * scale) * (value * value)
                root = jnp.maximum(two, tiny)
                part = one / (root * lax.rsqrt(root) + adam_eps)
                moved = part if moved is None else kept * moved + part
            moved_ref[:, where] = (inner_rate * moved).astype(jnp.bfloat16)
        one_out[:, where] = one
        two_out[:, where] = two

    chunked(columns, 512, body)


def adam(sums, gradients, one, two):
    short = jax.ShapeDtypeStruct(one.shape, jnp.bfloat16)
    whole = jax.ShapeDtypeStruct(one.shape, jnp.float32)
    return pl.pallas_call(
        adam_kernel,
        out_shape=(short,) * 4 + (whole,) * 2,
        in_specs=[VMEM] * 4,
        out_specs=(VMEM,) * 6,
        compiler_params=PARAMS,
        name="adam",
    )(sums, gradients, one, two)


def swapped(value, bit):
    size = lax.axis_size("rep")
    return lax.ppermute(value, "rep", [(r, r ^ (1 << bit)) for r in range(size)])


def mix_kernel(slow_ref, momentum_ref, moved_ref, other_slow_ref, other_moved_ref, *outs):
    shrink = 1.0 - kept**4

    def body(where):
        slow = slow_ref[:, where]
        other = other_slow_ref[:, where].astype(jnp.float32)
        moved = moved_ref[:, where].astype(jnp.float32)
        other_moved = other_moved_ref[:, where].astype(jnp.float32)
        average = 0.5 * (shrink * (slow + other) + (moved + other_moved))
        momentum = momentum_rate * momentum_ref[:, where] + average
        slow = slow + mix_rate * (other - slow) - outer_rate * (average + momentum_rate * momentum)
        outs[0][:, where] = slow
        outs[1][:, where] = momentum
        if len(outs) > 2:
            outs[2][:, where] = slow.astype(jnp.bfloat16)

    chunked(slow_ref.shape[1], 1024, body)


def mixed(last, *values):
    whole = jax.ShapeDtypeStruct(values[0].shape, jnp.float32)
    short = jax.ShapeDtypeStruct(values[0].shape, jnp.bfloat16)
    return pl.pallas_call(
        mix_kernel,
        out_shape=(whole,) * 2 + (() if last else (short,)),
        in_specs=[VMEM] * 5,
        out_specs=(VMEM,) * (2 if last else 3),
        compiler_params=PARAMS,
        name="mix",
    )(*values)


def first_part(bit, sums, sent, gradients, one, two):
    other_slow = swapped(sent, bit)
    sums = lax.all_to_all(sums, SHARD, 0, 0, tiled=True)
    return (other_slow, *adam(sums, gradients, one, two))


def second_part(order, slow, momentum, other_slow, *moved):
    other_moved = [swapped(part, bit) for part, bit in zip(moved, order)]
    for step, bit in enumerate(order):
        if step:
            other_slow = swapped(sent, bit)
        if step == 3:
            break
        slow, momentum, sent = mixed(
            False, slow, momentum, moved[step], other_slow, other_moved[step]
        )
    return slow, momentum, other_slow, other_moved[3]


def on_device(slow, momentum, one, two, gradients, pair_mask):
    slow, momentum, one, two = (v[0] for v in (slow, momentum, one, two))
    outer, inner, _, rows, columns = gradients.shape
    gradients = gradients.reshape(outer * inner, rows, columns)
    copies = 1
    for axis in SHARD:
        copies *= lax.axis_size(axis)
    branch, sums, sent = squares(pair_mask, gradients, slow, copies)
    other_slow, *moved, one, two = lax.switch(
        branch[0],
        [partial(first_part, bit) for bit in range(4)],
        sums, sent, gradients, one, two,
    )
    slow, momentum, other_slow, other_moved = lax.switch(
        branch[1],
        [partial(second_part, order) for order in permutations(range(4))],
        slow, momentum, other_slow, *moved,
    )
    slow, momentum = mixed(True, slow, momentum, moved[3], other_slow, other_moved)
    out = slow, momentum, one, two
    return tuple(v[None] for v in out)


def solution(mesh):
    finer = Mesh(
        mesh.devices.reshape(mesh.shape["rep"], 4, 4, 2), ("rep", "shard_0", "shard_1", "shard_2")
    )
    state = P("rep", SHARD, None)
    return jax.shard_map(
        on_device,
        mesh=finer,
        in_specs=(state,) * 4 + (P(None, None, "rep", SHARD, None), P()),
        out_specs=(state,) * 4,
        check_vma=False,
    )
```
